32 devices in a mesh: grp: 2 (over y), rx: 4 (over z), tw: 2 (over x), fq: 2 (over core).
Axes of the slice: x: 2, y: 2, z: 4, core: 2. Of those that a mesh axis runs over, the one named last changes fastest.
Arguments:
- traces: bfloat16 [8, 256, 15360], P('tw', ('grp', 'rx')), parts along dimension 1, may hold values from -48 to 48
- src_index: int32 [8, 64], P('grp'), parts along dimension 0, may hold values from 0 to 127
- valid: int32 [8, 256], P(None, 'grp'), parts along dimension 1, may hold values from 0 to 1, as said below
Outputs:
- correlations: bfloat16 [256, 256, 512], P(('tw', 'fq'), ('grp', 'rx')), parts along dimension 1
The draws below stay inside these ranges and needn't reach their ends.
There are 2 independent parts, one for each index of `grp`. The reference program is written for one: setup_inputs(seed, part) draws one part's arguments, and reference() takes and returns one part's arrays. A program takes and returns all parts, laid end to end along the dimension named above; each array names one. Nothing has to cross between parts.
Inputs may be any that keep to these rules, and one draw needn't show every extreme that they name: `valid`: some channels may be 0 in every window, and some windows 0 on every channel. `src_index`: A channel may be named by several sources.
All inputs are finite; a program needn't handle non-finite values.
Results may differ from the reference program's by a relative error of at most 0.0062.
Values may be sent and summed in bfloat16 or wider, within the bound.
No kernel may reach another device: no remote copies, remote signals or barrier semaphores. Data moves between devices by JAX's collectives and lax.ppermute only.
A program may use at most 128 MiB of HBM per device.

```python
import math
import jax
import jax.numpy as jnp
from jax import lax

NT = 15360
BAND = 512
F0 = 60
HW = 32
LAGS = 512
PANELS = 4
PANEL_CH = 64
SRC = 256
WINDOWS = 8
CHANNELS = 128


tone_count = 4


def draw_traces(key, part):
    sub_keys = jax.random.split(key, 5)
    sample_ids = jnp.arange(NT, dtype=jnp.int32)
    row_level = jnp.exp(jax.random.uniform(sub_keys[0], (1, CHANNELS, 1), minval=0.0, maxval=math.log(10.0)))
    noise_field = jnp.clip(jax.random.normal(sub_keys[1], (WINDOWS, CHANNELS, NT)), -4.0, 4.0)
    signal = noise_field * row_level
    tone_bins = jax.random.randint(sub_keys[2], (CHANNELS, tone_count), F0, F0 + BAND)
    tone_amp = jnp.exp(jax.random.uniform(sub_keys[3], (CHANNELS, tone_count), minval=math.log(0.05), maxval=0.0))
    tone_phase = jax.random.uniform(sub_keys[4], (WINDOWS, CHANNELS, tone_count), minval=-math.pi, maxval=math.pi)
    for tone_index in range(tone_count):
        phase_index = tone_bins[:, tone_index:tone_index + 1] * sample_ids[None, :] % NT
        angle_rad = phase_index.astype(jnp.float32) * (2.0 * math.pi / NT)
        weight_cos = (tone_amp[None, :, tone_index] * jnp.cos(tone_phase[:, :, tone_index]))[:, :, None]
        weight_sin = (tone_amp[None, :, tone_index] * jnp.sin(tone_phase[:, :, tone_index]))[:, :, None]
        signal = signal + weight_cos * jnp.cos(angle_rad)[None] - weight_sin * jnp.sin(angle_rad)[None]
    return signal.astype(jnp.bfloat16)


def draw_valid(key, part):
    sub_keys = jax.random.split(key, 3)
    window_ok = jax.random.randint(sub_keys[0], (WINDOWS, CHANNELS), 0, 4) > 0
    line_alive = jax.random.randint(sub_keys[1], (1, CHANNELS), 0, 24) > 0
    window_clean = jax.random.randint(sub_keys[2], (WINDOWS, 1), 0, 8) > 0
    return (window_ok & line_alive & window_clean).astype(jnp.int32)


def set_ends(entries, rng, smallest, largest):
    longest = entries.shape.index(max(entries.shape))
    spots = []
    for shift in (0, 1):
        where = [jax.random.randint(jax.random.fold_in(rng, axis), (), 0, length) for axis, length in enumerate(entries.shape)]
        where[longest] = (where[longest] + shift) % entries.shape[longest]
        spots.append(tuple(where))
    return entries.at[spots[0]].set(smallest).at[spots[1]].set(largest)


def setup_inputs(seed: int = 0, part: int = 0) -> dict:
    seeds = jax.random.split(jax.random.key(seed), 4)
    part_keys = jax.random.split(jax.random.fold_in(seeds[3], part), 4)
    return {
        "traces": draw_traces(jax.random.fold_in(jax.random.fold_in(seeds[3], part), 71), part),
        "src_index": set_ends(jax.random.randint(part_keys[1], (PANELS, PANEL_CH), 0, CHANNELS), jax.random.fold_in(part_keys[1], 1), 0, CHANNELS - 1).astype(jnp.int32),
        "valid": draw_valid(jax.random.fold_in(jax.random.fold_in(seeds[3], part), 71), part),
    }


two_pi = 2.0 * math.pi
eps_power = 1e-05
block_len = 1024

def coef_table(bin_ids):
    sample_ids = jnp.arange(block_len, dtype=jnp.int32)[:, None]
    phase_index = sample_ids * bin_ids[None, :] % NT
    angle_rad = phase_index.astype(jnp.float32) * (two_pi / NT)
    return jnp.concatenate([jnp.cos(angle_rad), -jnp.sin(angle_rad)], axis=1).astype(jnp.bfloat16)

def inverse_table(bin_ids):
    lag_shift = jnp.arange(LAGS, dtype=jnp.int32)[None, :] - LAGS // 2
    phase_index = bin_ids[:, None] * lag_shift % NT
    angle_rad = phase_index.astype(jnp.float32) * (two_pi / NT)
    return jnp.concatenate([jnp.cos(angle_rad), -jnp.sin(angle_rad)], axis=0).astype(jnp.bfloat16)

def window_box(width):
    row_ids = jnp.arange(width + 2 * HW, dtype=jnp.int32)[:, None]
    col_ids = jnp.arange(width, dtype=jnp.int32)[None, :]
    offset = row_ids - col_ids
    return ((offset >= 0) & (offset <= 2 * HW)).astype(jnp.float32)

def reference(traces, src_index, valid):
    bin_ids = F0 + jnp.arange(BAND, dtype=jnp.int32)
    trace_rows = traces.reshape(WINDOWS * CHANNELS, NT)
    base_table = coef_table(bin_ids)

    def add_block(turn_index, running):
        offset = (turn_index * block_len).astype(jnp.int32)
        trace_piece = lax.dynamic_slice_in_dim(trace_rows, offset, block_len, 1)
        partial_value = jnp.dot(trace_piece, base_table, preferred_element_type=jnp.float32)
        part_real = partial_value[:, :BAND]
        part_imag = partial_value[:, BAND:]
        phase_index = offset * bin_ids % NT
        angle_rad = phase_index.astype(jnp.float32) * (two_pi / NT)
        turn_real = jnp.cos(angle_rad)[None, :]
        turn_imag = -jnp.sin(angle_rad)[None, :]
        new_real = part_real * turn_real - part_imag * turn_imag
        new_imag = part_real * turn_imag + part_imag * turn_real
        return running + jnp.concatenate([new_real, new_imag], axis=1)
    spectrum = lax.fori_loop(0, NT // block_len, add_block, jnp.zeros((WINDOWS * CHANNELS, 2 * BAND), jnp.float32))
    spec_real = spectrum[:, :BAND]
    spec_imag = spectrum[:, BAND:]
    bin_power = spec_real * spec_real + spec_imag * spec_imag
    padded = jnp.pad(bin_power, ((0, 0), (HW, HW)))
    smooth = jnp.dot(padded, window_box(BAND), precision=lax.Precision.HIGHEST, preferred_element_type=jnp.float32) / (2 * HW + 1)
    white_gain = lax.rsqrt(smooth + eps_power)
    whitened = (spectrum * jnp.concatenate([white_gain, white_gain], axis=1)).astype(jnp.bfloat16)
    whitened = whitened.reshape(WINDOWS, CHANNELS, 2 * BAND)
    valid_float = valid.astype(jnp.float32)
    source_ids = src_index.reshape(SRC).astype(jnp.int32)
    source_valid = valid_float[:, source_ids]
    pair_count = jnp.dot(source_valid.T, valid_float, precision=lax.Precision.HIGHEST, preferred_element_type=jnp.float32)
    pair_floor = jnp.maximum(pair_count, 1.0)
    receivers = whitened.astype(jnp.float32) * valid_float[:, :, None]
    sources = whitened[:, source_ids, :].astype(jnp.float32) * source_valid[:, :, None]
    rec_real = receivers[..., :BAND]
    rec_imag = receivers[..., BAND:]
    src_panels = sources.reshape(WINDOWS, PANELS, PANEL_CH, 2 * BAND).transpose(1, 0, 2, 3)
    floor_panels = pair_floor.reshape(PANELS, PANEL_CH, CHANNELS)
    inv_table = inverse_table(bin_ids)
    inv_scale = 1.0 / math.sqrt(BAND)

    def one_panel(item):
        panel_src, panel_floor = item
        src_real = panel_src[..., :BAND]
        src_imag = panel_src[..., BAND:]
        pattern = 'wsx,wcx->scx'
        cross_real = jnp.einsum(pattern, src_real, rec_real, precision=lax.Precision.HIGHEST) + jnp.einsum(pattern, src_imag, rec_imag, precision=lax.Precision.HIGHEST)
        cross_imag = jnp.einsum(pattern, src_real, rec_imag, precision=lax.Precision.HIGHEST) - jnp.einsum(pattern, src_imag, rec_real, precision=lax.Precision.HIGHEST)
        stacked = (jnp.concatenate([cross_real, cross_imag], axis=2) / panel_floor[:, :, None]).astype(jnp.bfloat16)
        summed = jnp.dot(stacked.reshape(PANEL_CH * CHANNELS, 2 * BAND), inv_table, preferred_element_type=jnp.float32)
        return (summed * inv_scale).astype(jnp.bfloat16).reshape(PANEL_CH, CHANNELS, LAGS)
    result = lax.map(one_panel, (src_panels, floor_panels))
    return result.reshape(SRC, CHANNELS, LAGS)
```

```python
import math

import numpy as np
import jax
import jax.numpy as jnp
from jax import lax
from jax.experimental import pallas as pl
from jax.experimental.pallas import tpu as pltpu
from jax.sharding import PartitionSpec as P

NT = 15360
BAND = 512
F0 = 60
HW = 32
LAGS = 512
BLOCK = 1024
LANE = 128
KB = BAND // LANE
EPS = 1e-05


def tiled_columns(real, imag):
    rows = real.shape[0]
    pair = np.stack([real.reshape(rows, KB, LANE), imag.reshape(rows, KB, LANE)], axis=2)
    return pair.reshape(rows, 2 * BAND)


def forward_table():
    bins = F0 + np.arange(BAND)
    phase = np.arange(BLOCK)[:, None] * bins[None, :] % NT
    angle = phase * (2.0 * math.pi / NT)
    return tiled_columns(np.cos(angle), -np.sin(angle)).astype(jnp.bfloat16)


def turn_table():
    bins = F0 + np.arange(BAND)
    phase = BLOCK * np.arange(NT // BLOCK)[:, None] * bins[None, :] % NT
    angle = phase * (2.0 * math.pi / NT)
    return tiled_columns(np.cos(angle), -np.sin(angle)).astype(np.float32)


def inverse_table():
    bins = F0 + np.arange(BAND)
    phase = (np.arange(LAGS)[:, None] - LAGS // 2) * bins[None, :] % NT
    angle = phase * (2.0 * math.pi / NT)
    return np.ascontiguousarray(tiled_columns(np.cos(angle), -np.sin(angle)).T).astype(jnp.bfloat16)


def spectra_kernel(pos_ref, trace_ref, coef_ref, turn_ref, out_ref, spec_ref):
    step = pl.program_id(0)
    wins, chans, samples = trace_ref.shape
    rows = wins * chans
    blocks = samples // BLOCK
    pieces = [
        trace_ref[w, :, b * BLOCK : (b + 1) * BLOCK] for b in range(blocks) for w in range(wins)
    ]
    part = jnp.dot(
        jnp.concatenate(pieces, axis=0), coef_ref[...], preferred_element_type=jnp.float32
    )
    acc_re = part[:rows, :LANE]
    acc_im = part[:rows, LANE:]
    for b in range(1, blocks):
        re = part[b * rows : (b + 1) * rows, :LANE]
        im = part[b * rows : (b + 1) * rows, LANE:]
        turn_re = turn_ref[b : b + 1, :LANE]
        turn_im = turn_ref[b : b + 1, LANE:]
        acc_re = acc_re + (re * turn_re - im * turn_im)
        acc_im = acc_im + (re * turn_im + im * turn_re)
    spec_ref[step, 0] = acc_re
    spec_ref[step, 1] = acc_im

    @pl.when(step == KB - 1)
    def _():
        power = jnp.concatenate(
            [
                spec_ref[k, 0] * spec_ref[k, 0] + spec_ref[k, 1] * spec_ref[k, 1]
                for k in range(KB)
            ],
            axis=1,
        )
        high = power.astype(jnp.bfloat16)
        rest = power - high.astype(jnp.float32)
        middle = rest.astype(jnp.bfloat16)
        low = (rest - middle.astype(jnp.float32)).astype(jnp.bfloat16)
        row_ids = lax.broadcasted_iota(jnp.int32, (BAND, BAND), 0)
        col_ids = lax.broadcasted_iota(jnp.int32, (BAND, BAND), 1)
        box = jnp.where(jnp.abs(row_ids - col_ids) <= HW, 1.0, 0.0).astype(jnp.bfloat16)
        sums = jnp.dot(
            jnp.concatenate([high, middle, low], axis=0), box, preferred_element_type=jnp.float32
        )
        smooth = (sums[:rows] + (sums[rows : 2 * rows] + sums[2 * rows :])) / (2 * HW + 1)
        gain = lax.rsqrt(smooth + EPS)
        for k in range(KB):
            for p in range(2):
                white = spec_ref[k, p] * gain[:, k * LANE : (k + 1) * LANE]
                out_ref[:, :, (2 * k + p) * LANE : (2 * k + p + 1) * LANE] = white.astype(
                    jnp.bfloat16
                ).reshape(wins, chans, LANE)


def spectra(traces, fq_pos, fq_count):
    win_count, chans, samples = traces.shape
    wins = win_count // fq_count
    blocks = samples // BLOCK
    grid_spec = pltpu.PrefetchScalarGridSpec(
        num_scalar_prefetch=1,
        grid=(KB,),
        in_specs=[
            pl.BlockSpec((wins, chans, samples), lambda k, pos: (pos[0], 0, 0)),
            pl.BlockSpec((BLOCK, 2 * LANE), lambda k, pos: (0, k)),
            pl.BlockSpec((blocks, 2 * LANE), lambda k, pos: (0, k)),
        ],
        out_specs=pl.BlockSpec((wins, chans, 2 * BAND), lambda k, pos: (0, 0, 0)),
        scratch_shapes=[pltpu.VMEM((KB, 2, wins * chans, LANE), jnp.float32)],
    )
    return pl.pallas_call(
        spectra_kernel,
        grid_spec=grid_spec,
        out_shape=jax.ShapeDtypeStruct((wins, chans, 2 * BAND), jnp.bfloat16),
        name="spectra",
    )(fq_pos.reshape(1), traces, jnp.asarray(forward_table()), jnp.asarray(turn_table()))


def cross_kernel(sizes, *refs):
    groups, z_parts, wins, chans, src_local = sizes
    count = groups * z_parts
    block_refs = refs[:count]
    pick_ref, rate_ref, inv_ref, out_ref, src_ref, rec_ref, stack_ref = refs[count:]
    windows = groups * wins
    for g in range(groups):
        for w in range(wins):
            rows = jnp.concatenate(
                [
                    block_refs[g * z_parts + z][i * wins + w]
                    for z in range(z_parts)
                    for i in range(block_refs[g * z_parts + z].shape[0] // wins)
                ],
                axis=0,
            )
            chosen = jnp.dot(pick_ref[g * wins + w], rows, preferred_element_type=jnp.float32)
            for k in range(KB):
                re = chosen[:, 2 * k * LANE : (2 * k + 1) * LANE]
                im = chosen[:, (2 * k + 1) * LANE : (2 * k + 2) * LANE]
                s_re, s_im = re[:src_local], im[:src_local]
                r_re, r_im = re[src_local:], im[src_local:]
                src_ref[g * wins + w, k, 0] = s_re + s_im
                src_ref[g * wins + w, k, 1] = s_re
                src_ref[g * wins + w, k, 2] = s_im
                rec_ref[g * wins + w, k, 0] = r_re
                rec_ref[g * wins + w, k, 1] = r_im + r_re
                rec_ref[g * wins + w, k, 2] = r_im - r_re
    tiles = chans // 8

    def one_tile(index, carry):
        k = index // tiles
        tile = index % tiles
        rec = [
            [rec_ref[w, k, v, pl.ds(pl.multiple_of(tile * 8, 8), 8), :] for v in range(3)]
            for w in range(windows)
        ]

        def source_pair(pair, inner):
            both = []
            for half in range(2):
                s = pair * 2 + half
                sums = [None] * 3
                for w in range(windows):
                    for v in range(3):
                        row = src_ref[w, k, v, pl.ds(s, 8, stride=0), :]
                        term = row * rec[w][v]
                        sums[v] = term if w == 0 else sums[v] + term
                rate = rate_ref[s, pl.ds(pl.multiple_of(tile * 8, 8), 8), :]
                both.append(((sums[0] + sums[2]) * rate, (sums[1] - sums[0]) * rate))
            row = pl.multiple_of((pair * tiles + tile) * 16, 16)
            for p in range(2):
                stack_ref[2 * k + p, pl.ds(row, 16), :] = jnp.concatenate(
                    [both[0][p], both[1][p]], axis=0
                ).astype(jnp.bfloat16)
            return inner

        return lax.fori_loop(0, src_local // 2, source_pair, carry, unroll=2)

    lax.fori_loop(0, KB * tiles, one_tile, 0)
    scale = 1.0 / math.sqrt(BAND)
    chunk = min(8, src_local // 2)
    for first in range(0, src_local // 2, chunk):
        span = chunk * tiles * 16
        left = jnp.concatenate(
            [stack_ref[j, first * tiles * 16 : first * tiles * 16 + span, :] for j in range(2 * KB)],
            axis=1,
        )
        summed = jnp.dot(left, inv_ref[...], preferred_element_type=jnp.float32) * scale
        for i in range(chunk):
            for half in range(2):
                pieces = [
                    summed[((i * tiles + t) * 2 + half) * 8 : ((i * tiles + t) * 2 + half + 1) * 8]
                    for t in range(tiles)
                ]
                out_ref[2 * (first + i) + half] = jnp.concatenate(pieces, axis=0).astype(
                    jnp.bfloat16
                )


def shifted(value, axis, distance):
    count = lax.axis_size(axis)
    return lax.ppermute(value, axis, [(i, (i + distance) % count) for i in range(count)])


def shards(traces, src_index, valid):
    win_count, chans, _ = traces.shape
    rx_count, tw_count, fq_count = (lax.axis_size(a) for a in ("rx", "tw", "fq"))
    rx_pos, tw_pos, fq_pos = (lax.axis_index(a) for a in ("rx", "tw", "fq"))
    wins = win_count // fq_count
    own = spectra(traces, fq_pos, fq_count)

    along_z = [own] + [shifted(own, "rx", d) for d in range(1, rx_count)]
    if rx_count > 4:
        along_z = [jnp.concatenate(along_z, axis=0)]
    groups = [along_z]
    for d in range(1, tw_count):
        groups.append([shifted(v, "tw", d) for v in along_z])
    for d in range(1, fq_count):
        groups = groups + [[shifted(v, "fq", d) for v in g] for g in groups]
    z_parts = len(along_z)

    valid_float = valid.astype(jnp.float32)
    src_total = src_index.size
    src_local = src_total // (tw_count * fq_count)
    own_block = tw_pos * fq_count + fq_pos
    own_src = lax.dynamic_slice_in_dim(src_index.reshape(-1), own_block * src_local, src_local, 0)
    own_rec = rx_pos * chans + jnp.arange(chans, dtype=jnp.int32)
    wanted = jnp.concatenate([own_src, own_rec])
    channel_ids = (
        (rx_pos - jnp.arange(rx_count, dtype=jnp.int32)[:, None]) % rx_count * chans
        + jnp.arange(chans, dtype=jnp.int32)[None, :]
    ).reshape(-1)
    channel_total = rx_count * chans
    window_ids = []
    for f in range(fq_count):
        for t in range(tw_count):
            block = (tw_pos - t) % tw_count * fq_count + (fq_pos - f) % fq_count
            window_ids.append(block * wins + jnp.arange(wins, dtype=jnp.int32))
    window_ids = jnp.concatenate(window_ids)
    windows = window_ids.shape[0]
    use = (
        (window_ids[:, None] == jnp.arange(windows, dtype=jnp.int32)[None, :]).astype(jnp.float32)
        @ valid_float
    )
    spread = (wanted[:, None] == jnp.arange(channel_total, dtype=jnp.int32)[None, :]).astype(
        jnp.float32
    )
    use_wanted = jnp.dot(use, spread.T, preferred_element_type=jnp.float32)
    pick = jnp.where(
        wanted[None, :, None] == channel_ids[None, None, :], use_wanted[:, :, None], 0.0
    ).astype(jnp.bfloat16)
    pair_count = jnp.dot(
        use_wanted[:, :src_local].T, use_wanted[:, src_local:], preferred_element_type=jnp.float32
    )
    rate = jnp.broadcast_to(
        (1.0 / jnp.maximum(pair_count, 1.0))[:, :, None], (src_local, chans, LANE)
    )

    operands = [v for g in groups for v in g]
    sizes = (len(groups), z_parts, wins, chans, src_local)
    return pl.pallas_call(
        lambda *refs: cross_kernel(sizes, *refs),
        out_shape=jax.ShapeDtypeStruct((src_local, chans, LAGS), jnp.bfloat16),
        scratch_shapes=[
            pltpu.VMEM((windows, KB, 3, src_local, LANE), jnp.float32),
            pltpu.VMEM((windows, KB, 3, chans, LANE), jnp.float32),
            pltpu.VMEM((2 * KB, src_local * chans, LANE), jnp.bfloat16),
        ],
        name="cross",
    )(*operands, pick, rate, jnp.asarray(inverse_table()))


def solution(mesh):
    return jax.shard_map(
        shards,
        mesh=mesh,
        in_specs=(P("tw", ("grp", "rx"), None), P("grp", None), P(None, "grp")),
        out_specs=P(("tw", "fq"), ("grp", "rx"), None),
        check_vma=False,
    )
```

```python
import math

import numpy as np
import jax
import jax.numpy as jnp
from jax import lax
from jax.experimental import pallas as pl
from jax.experimental.pallas import tpu as pltpu
from jax.sharding import PartitionSpec as P

NT = 15360
BAND = 512
F0 = 60
HW = 32
LAGS = 512
BLOCK = 1024
LANE = 128
KB = BAND // LANE
SPLIT = 2
LIMIT = 40 * 2**20
EPS = 1e-05


def tiled_columns(real, imag):
    rows = real.shape[0]
    pair = np.stack([real.reshape(rows, KB, LANE), imag.reshape(rows, KB, LANE)], axis=2)
    return pair.reshape(rows, 2 * BAND)


def forward_table():
    bins = F0 + np.arange(BAND)
    phase = np.arange(BLOCK)[:, None] * bins[None, :] % NT
    angle = phase * (2.0 * math.pi / NT)
    return tiled_columns(np.cos(angle), -np.sin(angle)).astype(jnp.bfloat16)


def turn_table():
    bins = F0 + np.arange(BAND)
    phase = BLOCK * np.arange(NT // BLOCK)[:, None] * bins[None, :] % NT
    angle = phase * (2.0 * math.pi / NT)
    return tiled_columns(np.cos(angle), -np.sin(angle)).astype(np.float32)


def inverse_table():
    bins = F0 + np.arange(BAND)
    phase = (np.arange(LAGS)[:, None] - LAGS // 2) * bins[None, :] % NT
    angle = phase * (2.0 * math.pi / NT)
    return np.ascontiguousarray(tiled_columns(np.cos(angle), -np.sin(angle)).T).astype(jnp.bfloat16)


def spectra_kernel(pos_ref, trace_ref, coef_ref, turn_ref, out_ref, spec_ref):
    step = pl.program_id(0)
    wins, chans, samples = trace_ref.shape
    rows = wins * chans
    blocks = samples // BLOCK
    pieces = [
        trace_ref[w, :, b * BLOCK : (b + 1) * BLOCK] for b in range(blocks) for w in range(wins)
    ]
    part = jnp.dot(
        jnp.concatenate(pieces, axis=0), coef_ref[...], preferred_element_type=jnp.float32
    )
    acc_re = part[:rows, :LANE]
    acc_im = part[:rows, LANE:]
    for b in range(1, blocks):
        re = part[b * rows : (b + 1) * rows, :LANE]
        im = part[b * rows : (b + 1) * rows, LANE:]
        turn_re = turn_ref[b : b + 1, :LANE]
        turn_im = turn_ref[b : b + 1, LANE:]
        acc_re = acc_re + (re * turn_re - im * turn_im)
        acc_im = acc_im + (re * turn_im + im * turn_re)
    spec_ref[step, 0] = acc_re
    spec_ref[step, 1] = acc_im

    @pl.when(step == KB - 1)
    def _():
        power = jnp.concatenate(
            [
                spec_ref[k, 0] * spec_ref[k, 0] + spec_ref[k, 1] * spec_ref[k, 1]
                for k in range(KB)
            ],
            axis=1,
        )
        high = power.astype(jnp.bfloat16)
        rest = power - high.astype(jnp.float32)
        middle = rest.astype(jnp.bfloat16)
        low = (rest - middle.astype(jnp.float32)).astype(jnp.bfloat16)
        row_ids = lax.broadcasted_iota(jnp.int32, (BAND, BAND), 0)
        col_ids = lax.broadcasted_iota(jnp.int32, (BAND, BAND), 1)
        box = jnp.where(jnp.abs(row_ids - col_ids) <= HW, 1.0, 0.0).astype(jnp.bfloat16)
        sums = jnp.dot(
            jnp.concatenate([high, middle, low], axis=0), box, preferred_element_type=jnp.float32
        )
        smooth = (sums[:rows] + (sums[rows : 2 * rows] + sums[2 * rows :])) / (2 * HW + 1)
        gain = lax.rsqrt(smooth + EPS)
        for k in range(KB):
            for p in range(2):
                white = spec_ref[k, p] * gain[:, k * LANE : (k + 1) * LANE]
                out_ref[:, :, (2 * k + p) * LANE : (2 * k + p + 1) * LANE] = white.astype(
                    jnp.bfloat16
                ).reshape(wins, chans, LANE)


def spectra(traces, fq_pos, fq_count):
    win_count, chans, samples = traces.shape
    wins = win_count // fq_count
    blocks = samples // BLOCK
    grid_spec = pltpu.PrefetchScalarGridSpec(
        num_scalar_prefetch=1,
        grid=(KB,),
        in_specs=[
            pl.BlockSpec((wins, chans, samples), lambda k, pos: (pos[0], 0, 0)),
            pl.BlockSpec((BLOCK, 2 * LANE), lambda k, pos: (0, k)),
            pl.BlockSpec((blocks, 2 * LANE), lambda k, pos: (0, k)),
        ],
        out_specs=pl.BlockSpec((wins, chans, 2 * BAND), lambda k, pos: (0, 0, 0)),
        scratch_shapes=[pltpu.VMEM((KB, 2, wins * chans, LANE), jnp.float32)],
    )
    return pl.pallas_call(
        spectra_kernel,
        grid_spec=grid_spec,
        out_shape=jax.ShapeDtypeStruct((wins, chans, 2 * BAND), jnp.bfloat16),
        name="spectra",
    )(fq_pos.reshape(1), traces, jnp.asarray(forward_table()), jnp.asarray(turn_table()))


def choose_rows(block_refs, pick_ref, src_ref, rec_ref, sizes, k):
    groups, z_parts, wins, _, src_local = sizes
    lanes = slice(k * 2 * LANE, (k + 1) * 2 * LANE)
    for g in range(groups):
        for w in range(wins):
            rows = jnp.concatenate(
                [
                    block_refs[g * z_parts + z][i * wins + w, :, lanes]
                    for z in range(z_parts)
                    for i in range(block_refs[g * z_parts + z].shape[0] // wins)
                ],
                axis=0,
            )
            chosen = jnp.dot(pick_ref[g * wins + w], rows, preferred_element_type=jnp.float32)
            re, im = chosen[:, :LANE], chosen[:, LANE:]
            s_re, s_im = re[:src_local], im[:src_local]
            r_re, r_im = re[src_local:], im[src_local:]
            src_ref[g * wins + w, 0] = s_re + s_im
            src_ref[g * wins + w, 1] = s_re
            src_ref[g * wins + w, 2] = s_im
            rec_ref[g * wins + w, 0] = r_re
            rec_ref[g * wins + w, 1] = r_im + r_re
            rec_ref[g * wins + w, 2] = r_im - r_re


def cross_sums(src_ref, s, recs):
    sums = [[None] * 3 for _ in recs]
    for w in range(len(recs[0])):
        for v in range(3):
            row = src_ref[w, v, pl.ds(s, 8, stride=0), :]
            for total, rec in zip(sums, recs):
                term = row * rec[w][v]
                total[v] = term if w == 0 else total[v] + term
    return [(total[0] + total[2], total[1] - total[0]) for total in sums]


def receiver_tiles(rec_ref, windows, pair):
    spans = [pl.ds(pl.multiple_of(pair * 16 + half * 8, 8), 8) for half in range(2)]
    recs = [
        [[rec_ref[w, v, span, :] for v in range(3)] for w in range(windows)] for span in spans
    ]
    return spans, recs


def partial_kernel(sizes, first, last, *refs):
    groups, z_parts, wins, chans, src_local = sizes
    count = groups * z_parts
    pick_ref, out_ref, src_ref, rec_ref = refs[count:]
    windows = groups * wins
    for k in range(first, last):
        choose_rows(refs[:count], pick_ref, src_ref, rec_ref, sizes, k)

        def one_pair(pair, carry):
            spans, recs = receiver_tiles(rec_ref, windows, pair)

            def one_source(s, inner):
                for span, sums in zip(spans, cross_sums(src_ref, s, recs)):
                    for p in range(2):
                        out_ref[k - first, s, p, span, :] = sums[p]
                return inner

            return lax.fori_loop(0, src_local, one_source, carry, unroll=8)

        lax.fori_loop(0, chans // 16, one_pair, 0)


def final_kernel(sizes, firsts, *refs):
    groups, z_parts, wins, chans, src_local = sizes
    count = groups * z_parts
    parts = len(firsts)
    part_refs = refs[count : count + parts]
    pick_ref, rate_ref, inv_ref, out_ref = refs[count + parts : count + parts + 4]
    src_ref, rec_ref, stack_ref, stage_ref, sems = refs[count + parts + 4 :]
    windows = groups * wins
    pairs = chans // 16
    for k in range(KB):
        choose_rows(refs[:count], pick_ref, src_ref, rec_ref, sizes, k)
        index = max(i for i in range(parts) if firsts[i] <= k)
        part_ref, part_k = part_refs[index], k - firsts[index]

        def one_pair(pair, carry):
            spans, recs = receiver_tiles(rec_ref, windows, pair)

            def one_source(s, inner):
                sums = cross_sums(src_ref, s, recs)
                row = pl.multiple_of((s * pairs + pair) * 16, 16)
                for p in range(2):
                    both = [
                        (total[p] + part_ref[part_k, s, p, span, :]) * rate_ref[s, span, :]
                        for total, span in zip(sums, spans)
                    ]
                    stack_ref[2 * k + p, pl.ds(row, 16), :] = jnp.concatenate(
                        both, axis=0
                    ).astype(jnp.bfloat16)
                return inner

            return lax.fori_loop(0, src_local, one_source, carry, unroll=8)

        lax.fori_loop(0, pairs, one_pair, 0)
    scale = 1.0 / math.sqrt(BAND)
    chunk = min(16, src_local)
    copies = []
    for index, first in enumerate(range(0, src_local, chunk)):
        span = slice(first * chans, (first + chunk) * chans)
        left = jnp.concatenate([stack_ref[j, span, :] for j in range(2 * KB)], axis=1)
        summed = jnp.dot(left, inv_ref[...], preferred_element_type=jnp.float32) * scale
        stage_ref[first : first + chunk] = summed.astype(jnp.bfloat16).reshape(chunk, chans, LAGS)
        copies.append(
            pltpu.make_async_copy(
                stage_ref.at[pl.ds(first, chunk)], out_ref.at[pl.ds(first, chunk)], sems.at[index]
            )
        )
        copies[-1].start()
    for copy in copies:
        copy.wait()


def held(values):
    small = sum(v.size * v.dtype.itemsize for v in values) <= 24 * 2**20
    return [pl.BlockSpec(memory_space=pltpu.VMEM) if small else pl.BlockSpec()] * len(values)


def work_space(sizes):
    groups, _, wins, chans, src_local = sizes
    return [
        pltpu.VMEM((groups * wins, 3, src_local, LANE), jnp.float32),
        pltpu.VMEM((groups * wins, 3, chans, LANE), jnp.float32),
    ]


def partial_cross(sizes, blocks, pick, first, last):
    chans, src_local = sizes[3:]
    operands = (*blocks, pick)
    return pl.pallas_call(
        lambda *refs: partial_kernel(sizes, first, last, *refs),
        in_specs=held(operands),
        out_specs=pl.BlockSpec(memory_space=pltpu.VMEM),
        out_shape=jax.ShapeDtypeStruct((last - first, src_local, 2, chans, LANE), jnp.float32),
        scratch_shapes=work_space(sizes),
        compiler_params=pltpu.CompilerParams(vmem_limit_bytes=LIMIT),
    )(*operands)


def final_cross(sizes, blocks, parts, firsts, pick, rate):
    chans, src_local = sizes[3:]
    operands = (*blocks, *parts, pick, rate, jnp.asarray(inverse_table()))
    chunks = src_local // min(16, src_local)
    return pl.pallas_call(
        lambda *refs: final_kernel(sizes, firsts, *refs),
        in_specs=held(operands),
        out_specs=pl.BlockSpec(memory_space=pl.ANY),
        out_shape=jax.ShapeDtypeStruct((src_local, chans, LAGS), jnp.bfloat16),
        scratch_shapes=work_space(sizes)
        + [
            pltpu.VMEM((2 * KB, src_local * chans, LANE), jnp.bfloat16),
            pltpu.VMEM((src_local, chans, LAGS), jnp.bfloat16),
            pltpu.SemaphoreType.DMA((chunks,)),
        ],
        compiler_params=pltpu.CompilerParams(vmem_limit_bytes=LIMIT),
        name="cross",
    )(*operands)


def exchanged(value, axis, distance):
    count = lax.axis_size(axis)
    return lax.ppermute(value, axis, [(i, i ^ distance) for i in range(count)])


def whole_step(traces, src_index, valid):
    win_count, chans, _ = traces.shape
    rx_count, tw_count, fq_count = (lax.axis_size(a) for a in ("rx", "tw", "fq"))
    rx_pos, tw_pos, fq_pos = (lax.axis_index(a) for a in ("rx", "tw", "fq"))
    wins = win_count // fq_count
    own = spectra(traces, fq_pos, fq_count)

    along_z = [own] + [exchanged(own, "rx", d) for d in range(1, rx_count)]
    if rx_count > 4:
        along_z = [jnp.concatenate(along_z, axis=0)]
    near = [along_z]
    for d in range(1, fq_count):
        near.append([exchanged(v, "fq", d) for v in along_z])
    far = []
    for t in range(1, tw_count):
        far.append([exchanged(v, "tw", t) for v in along_z])
        for d in range(1, fq_count):
            far.append([exchanged(v, "fq", d) for v in far[-1]])
    z_parts = len(along_z)

    valid_float = valid.astype(jnp.float32)
    src_total = src_index.size
    src_local = src_total // (tw_count * fq_count)
    own_block = tw_pos * fq_count + fq_pos
    own_src = lax.dynamic_slice_in_dim(src_index.reshape(-1), own_block * src_local, src_local, 0)
    own_rec = rx_pos * chans + jnp.arange(chans, dtype=jnp.int32)
    wanted = jnp.concatenate([own_src, own_rec])
    channel_ids = (
        (rx_pos ^ jnp.arange(rx_count, dtype=jnp.int32)[:, None]) * chans
        + jnp.arange(chans, dtype=jnp.int32)[None, :]
    ).reshape(-1)
    channel_total = rx_count * chans
    window_ids = []
    for t in range(tw_count):
        for f in range(fq_count):
            block = (tw_pos ^ t) * fq_count + (fq_pos ^ f)
            window_ids.append(block * wins + jnp.arange(wins, dtype=jnp.int32))
    window_ids = jnp.concatenate(window_ids)
    windows = window_ids.shape[0]
    use = (
        (window_ids[:, None] == jnp.arange(windows, dtype=jnp.int32)[None, :]).astype(jnp.float32)
        @ valid_float
    )
    spread = (wanted[:, None] == jnp.arange(channel_total, dtype=jnp.int32)[None, :]).astype(
        jnp.float32
    )
    use_wanted = jnp.dot(use, spread.T, preferred_element_type=jnp.float32)
    pick = jnp.where(
        wanted[None, :, None] == channel_ids[None, None, :], use_wanted[:, :, None], 0.0
    ).astype(jnp.bfloat16)
    pair_count = jnp.dot(
        use_wanted[:, :src_local].T, use_wanted[:, src_local:], preferred_element_type=jnp.float32
    )
    rate = jnp.broadcast_to(
        (1.0 / jnp.maximum(pair_count, 1.0))[:, :, None], (src_local, chans, LANE)
    )

    near_windows = len(near) * wins
    sizes = (len(near), z_parts, wins, chans, src_local)
    near_blocks = [v for g in near for v in g]
    firsts = (0, SPLIT)
    parts = []
    for first, last in zip(firsts, (*firsts[1:], KB)):
        parts.append(partial_cross(sizes, near_blocks, pick[:near_windows], first, last))
    sizes = (len(far), z_parts, wins, chans, src_local)
    far_blocks = [v for g in far for v in g]
    return final_cross(sizes, far_blocks, parts, firsts, pick[near_windows:], rate)


def solution(mesh):
    return jax.shard_map(
        whole_step,
        mesh=mesh,
        in_specs=(P("tw", ("grp", "rx"), None), P("grp", None), P(None, "grp")),
        out_specs=P(("tw", "fq"), ("grp", "rx"), None),
        check_vma=False,
    )
```

```python
import math

import numpy as np
import jax
import jax.numpy as jnp
from jax import lax
from jax.experimental import pallas as pl
from jax.experimental.pallas import tpu as pltpu
from jax.sharding import PartitionSpec as P

NT = 15360
BAND = 512
F0 = 60
HW = 32
LAGS = 512
BLOCK = 1024
LANE = 128
KB = BAND // LANE
SPLIT = 2
EPS = 1e-05


def tiled_columns(real, imag):
    rows = real.shape[0]
    pair = np.stack([real.reshape(rows, KB, LANE), imag.reshape(rows, KB, LANE)], axis=2)
    return pair.reshape(rows, 2 * BAND)


def forward_table():
    bins = F0 + np.arange(BAND)
    phase = np.arange(BLOCK)[:, None] * bins[None, :] % NT
    angle = phase * (2.0 * math.pi / NT)
    return tiled_columns(np.cos(angle), -np.sin(angle)).astype(jnp.bfloat16)


def turn_table():
    bins = F0 + np.arange(BAND)
    phase = BLOCK * np.arange(NT // BLOCK)[:, None] * bins[None, :] % NT
    angle = phase * (2.0 * math.pi / NT)
    return tiled_columns(np.cos(angle), -np.sin(angle)).astype(np.float32)


def inverse_table():
    bins = F0 + np.arange(BAND)
    phase = (np.arange(LAGS)[:, None] - LAGS // 2) * bins[None, :] % NT
    angle = phase * (2.0 * math.pi / NT)
    return np.ascontiguousarray(tiled_columns(np.cos(angle), -np.sin(angle)).T).astype(jnp.bfloat16)


def spectra_kernel(pos_ref, trace_ref, coef_ref, turn_ref, out_ref, spec_ref):
    step = pl.program_id(0)
    wins, chans, samples = trace_ref.shape
    rows = wins * chans
    blocks = samples // BLOCK
    pieces = [
        trace_ref[w, :, b * BLOCK : (b + 1) * BLOCK] for b in range(blocks) for w in range(wins)
    ]
    part = jnp.dot(
        jnp.concatenate(pieces, axis=0), coef_ref[...], preferred_element_type=jnp.float32
    )
    acc_re = part[:rows, :LANE]
    acc_im = part[:rows, LANE:]
    for b in range(1, blocks):
        re = part[b * rows : (b + 1) * rows, :LANE]
        im = part[b * rows : (b + 1) * rows, LANE:]
        turn_re = turn_ref[b : b + 1, :LANE]
        turn_im = turn_ref[b : b + 1, LANE:]
        acc_re = acc_re + (re * turn_re - im * turn_im)
        acc_im = acc_im + (re * turn_im + im * turn_re)
    spec_ref[step, 0] = acc_re
    spec_ref[step, 1] = acc_im

    @pl.when(step == KB - 1)
    def _():
        power = jnp.concatenate(
            [
                spec_ref[k, 0] * spec_ref[k, 0] + spec_ref[k, 1] * spec_ref[k, 1]
                for k in range(KB)
            ],
            axis=1,
        )
        high = power.astype(jnp.bfloat16)
        rest = power - high.astype(jnp.float32)
        middle = rest.astype(jnp.bfloat16)
        low = (rest - middle.astype(jnp.float32)).astype(jnp.bfloat16)
        row_ids = lax.broadcasted_iota(jnp.int32, (BAND, BAND), 0)
        col_ids = lax.broadcasted_iota(jnp.int32, (BAND, BAND), 1)
        box = jnp.where(jnp.abs(row_ids - col_ids) <= HW, 1.0, 0.0).astype(jnp.bfloat16)
        sums = jnp.dot(
            jnp.concatenate([high, middle, low], axis=0), box, preferred_element_type=jnp.float32
        )
        smooth = (sums[:rows] + (sums[rows : 2 * rows] + sums[2 * rows :])) / (2 * HW + 1)
        gain = lax.rsqrt(smooth + EPS)
        for k in range(KB):
            for p in range(2):
                white = spec_ref[k, p] * gain[:, k * LANE : (k + 1) * LANE]
                out_ref[:, :, (2 * k + p) * LANE : (2 * k + p + 1) * LANE] = white.astype(
                    jnp.bfloat16
                ).reshape(wins, chans, LANE)


def spectra(traces, fq_pos, fq_count):
    win_count, chans, samples = traces.shape
    wins = win_count // fq_count
    blocks = samples // BLOCK
    grid_spec = pltpu.PrefetchScalarGridSpec(
        num_scalar_prefetch=1,
        grid=(KB,),
        in_specs=[
            pl.BlockSpec((wins, chans, samples), lambda k, pos: (pos[0], 0, 0)),
            pl.BlockSpec((BLOCK, 2 * LANE), lambda k, pos: (0, k)),
            pl.BlockSpec((blocks, 2 * LANE), lambda k, pos: (0, k)),
        ],
        out_specs=pl.BlockSpec((wins, chans, 2 * BAND), lambda k, pos: (0, 0, 0)),
        scratch_shapes=[pltpu.VMEM((KB, 2, wins * chans, LANE), jnp.float32)],
    )
    return pl.pallas_call(
        spectra_kernel,
        grid_spec=grid_spec,
        out_shape=jax.ShapeDtypeStruct((wins, chans, 2 * BAND), jnp.bfloat16),
        name="spectra",
    )(fq_pos.reshape(1), traces, jnp.asarray(forward_table()), jnp.asarray(turn_table()))


def choose_rows(block_refs, pick_ref, src_ref, rec_ref, sizes, k):
    groups, z_parts, wins, _, src_local = sizes
    lanes = slice(k * 2 * LANE, (k + 1) * 2 * LANE)
    for g in range(groups):
        for w in range(wins):
            rows = jnp.concatenate(
                [
                    block_refs[g * z_parts + z][i * wins + w, :, lanes]
                    for z in range(z_parts)
                    for i in range(block_refs[g * z_parts + z].shape[0] // wins)
                ],
                axis=0,
            )
            chosen = jnp.dot(pick_ref[g * wins + w], rows, preferred_element_type=jnp.float32)
            re, im = chosen[:, :LANE], chosen[:, LANE:]
            s_re, s_im = re[:src_local], im[:src_local]
            r_re, r_im = re[src_local:], im[src_local:]
            src_ref[g * wins + w, 0] = s_re + s_im
            src_ref[g * wins + w, 1] = s_re
            src_ref[g * wins + w, 2] = s_im
            rec_ref[g * wins + w, 0] = r_re
            rec_ref[g * wins + w, 1] = r_im + r_re
            rec_ref[g * wins + w, 2] = r_im - r_re


def cross_sums(src_ref, s, recs):
    sums = [[None] * 3 for _ in recs]
    for w in range(len(recs[0])):
        for v in range(3):
            row = src_ref[w, v, pl.ds(s, 8, stride=0), :]
            for total, rec in zip(sums, recs):
                term = row * rec[w][v]
                total[v] = term if w == 0 else total[v] + term
    return [(total[0] + total[2], total[1] - total[0]) for total in sums]


def receiver_tiles(rec_ref, windows, pair):
    spans = [pl.ds(pl.multiple_of(pair * 16 + half * 8, 8), 8) for half in range(2)]
    recs = [
        [[rec_ref[w, v, span, :] for v in range(3)] for w in range(windows)] for span in spans
    ]
    return spans, recs


def partial_kernel(sizes, first, last, *refs):
    groups, z_parts, wins, chans, src_local = sizes
    count = groups * z_parts
    pick_ref, out_ref, src_ref, rec_ref = refs[count:]
    windows = groups * wins
    for k in range(first, last):
        choose_rows(refs[:count], pick_ref, src_ref, rec_ref, sizes, k)

        def one_pair(pair, carry):
            spans, recs = receiver_tiles(rec_ref, windows, pair)

            def one_source(s, inner):
                for span, sums in zip(spans, cross_sums(src_ref, s, recs)):
                    for p in range(2):
                        out_ref[k - first, s, p, span, :] = sums[p]
                return inner

            return lax.fori_loop(0, src_local, one_source, carry, unroll=16)

        lax.fori_loop(0, chans // 16, one_pair, 0)


def final_kernel(sizes, firsts, *refs):
    groups, z_parts, wins, chans, src_local = sizes
    count = groups * z_parts
    parts = len(firsts)
    part_refs = refs[count : count + parts]
    pick_ref, rate_ref, inv_ref, out_ref = refs[count + parts : count + parts + 4]
    src_ref, rec_ref, stack_ref, stage_ref, sems = refs[count + parts + 4 :]
    windows = groups * wins
    pairs = chans // 16
    for k in range(KB):
        choose_rows(refs[:count], pick_ref, src_ref, rec_ref, sizes, k)
        index = max(i for i in range(parts) if firsts[i] <= k)
        part_ref, part_k = part_refs[index], k - firsts[index]

        def one_pair(pair, carry):
            spans, recs = receiver_tiles(rec_ref, windows, pair)

            def one_source(s, inner):
                sums = cross_sums(src_ref, s, recs)
                row = pl.multiple_of((s * pairs + pair) * 16, 16)
                for p in range(2):
                    both = [
                        (total[p] + part_ref[part_k, s, p, span, :]) * rate_ref[s, span, :]
                        for total, span in zip(sums, spans)
                    ]
                    stack_ref[2 * k + p, pl.ds(row, 16), :] = jnp.concatenate(
                        both, axis=0
                    ).astype(jnp.bfloat16)
                return inner

            return lax.fori_loop(0, src_local, one_source, carry, unroll=16)

        lax.fori_loop(0, pairs, one_pair, 0)
    scale = 1.0 / math.sqrt(BAND)
    chunk = min(16, src_local)
    copies = []
    for index, first in enumerate(range(0, src_local, chunk)):
        span = slice(first * chans, (first + chunk) * chans)
        left = jnp.concatenate([stack_ref[j, span, :] for j in range(2 * KB)], axis=1)
        summed = jnp.dot(left, inv_ref[...], preferred_element_type=jnp.float32) * scale
        stage_ref[first : first + chunk] = summed.astype(jnp.bfloat16).reshape(chunk, chans, LAGS)
        copies.append(
            pltpu.make_async_copy(
                stage_ref.at[pl.ds(first, chunk)], out_ref.at[pl.ds(first, chunk)], sems.at[index]
            )
        )
        copies[-1].start()
    for copy in copies:
        copy.wait()


def held(values):
    small = sum(v.size * v.dtype.itemsize for v in values) <= 16 * 2**20
    specs = [pl.BlockSpec(memory_space=pltpu.VMEM) if small else pl.BlockSpec()] * len(values)
    return specs, pltpu.CompilerParams(vmem_limit_bytes=(16 if small else 48) * 2**20)


def work_space(sizes):
    groups, _, wins, chans, src_local = sizes
    return [
        pltpu.VMEM((groups * wins, 3, src_local, LANE), jnp.float32),
        pltpu.VMEM((groups * wins, 3, chans, LANE), jnp.float32),
    ]


def partial_cross(sizes, blocks, pick, first, last):
    chans, src_local = sizes[3:]
    operands = (*blocks, pick)
    specs, params = held(operands)
    return pl.pallas_call(
        lambda *refs: partial_kernel(sizes, first, last, *refs),
        in_specs=specs,
        out_specs=pl.BlockSpec(memory_space=pltpu.VMEM),
        out_shape=jax.ShapeDtypeStruct((last - first, src_local, 2, chans, LANE), jnp.float32),
        scratch_shapes=work_space(sizes),
        compiler_params=params,
    )(*operands)


def final_cross(sizes, blocks, parts, firsts, pick, rate):
    chans, src_local = sizes[3:]
    operands = (*blocks, *parts, pick, rate, jnp.asarray(inverse_table()))
    chunks = src_local // min(16, src_local)
    specs, params = held(operands)
    return pl.pallas_call(
        lambda *refs: final_kernel(sizes, firsts, *refs),
        in_specs=specs,
        out_specs=pl.BlockSpec(memory_space=pl.ANY),
        out_shape=jax.ShapeDtypeStruct((src_local, chans, LAGS), jnp.bfloat16),
        scratch_shapes=work_space(sizes)
        + [
            pltpu.VMEM((2 * KB, src_local * chans, LANE), jnp.bfloat16),
            pltpu.VMEM((src_local, chans, LAGS), jnp.bfloat16),
            pltpu.SemaphoreType.DMA((chunks,)),
        ],
        compiler_params=params,
        name="cross",
    )(*operands)


def exchanged(value, axis, distance):
    count = lax.axis_size(axis)
    return lax.ppermute(value, axis, [(i, i ^ distance) for i in range(count)])


def whole_step(traces, src_index, valid):
    win_count, chans, _ = traces.shape
    rx_count, tw_count, fq_count = (lax.axis_size(a) for a in ("rx", "tw", "fq"))
    rx_pos, tw_pos, fq_pos = (lax.axis_index(a) for a in ("rx", "tw", "fq"))
    wins = win_count // fq_count
    own = spectra(traces, fq_pos, fq_count)

    along_z = [own] + [exchanged(own, "rx", d) for d in range(1, rx_count)]
    if rx_count > 4:
        along_z = [jnp.concatenate(along_z, axis=0)]
    near = [along_z]
    for d in range(1, fq_count):
        near.append([exchanged(v, "fq", d) for v in along_z])
    far = []
    for t in range(1, tw_count):
        far.append([exchanged(v, "tw", t) for v in along_z])
        for d in range(1, fq_count):
            far.append([exchanged(v, "fq", d) for v in far[-1]])
    z_parts = len(along_z)

    valid_float = valid.astype(jnp.float32)
    src_total = src_index.size
    src_local = src_total // (tw_count * fq_count)
    own_block = tw_pos * fq_count + fq_pos
    own_src = lax.dynamic_slice_in_dim(src_index.reshape(-1), own_block * src_local, src_local, 0)
    own_rec = rx_pos * chans + jnp.arange(chans, dtype=jnp.int32)
    wanted = jnp.concatenate([own_src, own_rec])
    channel_ids = (
        (rx_pos ^ jnp.arange(rx_count, dtype=jnp.int32)[:, None]) * chans
        + jnp.arange(chans, dtype=jnp.int32)[None, :]
    ).reshape(-1)
    channel_total = rx_count * chans
    window_ids = []
    for t in range(tw_count):
        for f in range(fq_count):
            block = (tw_pos ^ t) * fq_count + (fq_pos ^ f)
            window_ids.append(block * wins + jnp.arange(wins, dtype=jnp.int32))
    window_ids = jnp.concatenate(window_ids)
    windows = window_ids.shape[0]
    use = (
        (window_ids[:, None] == jnp.arange(windows, dtype=jnp.int32)[None, :]).astype(jnp.float32)
        @ valid_float
    )
    spread = (wanted[:, None] == jnp.arange(channel_total, dtype=jnp.int32)[None, :]).astype(
        jnp.float32
    )
    use_wanted = jnp.dot(use, spread.T, preferred_element_type=jnp.float32)
    pick = jnp.where(
        wanted[None, :, None] == channel_ids[None, None, :], use_wanted[:, :, None], 0.0
    ).astype(jnp.bfloat16)
    pair_count = jnp.dot(
        use_wanted[:, :src_local].T, use_wanted[:, src_local:], preferred_element_type=jnp.float32
    )
    rate = jnp.broadcast_to(
        (1.0 / jnp.maximum(pair_count, 1.0))[:, :, None], (src_local, chans, LANE)
    )

    pick, rate = lax.optimization_barrier((pick, rate))
    near_windows = len(near) * wins
    sizes = (len(near), z_parts, wins, chans, src_local)
    near_blocks = [v for g in near for v in g]
    firsts = (0, SPLIT)
    parts = []
    for first, last in zip(firsts, (*firsts[1:], KB)):
        parts.append(partial_cross(sizes, near_blocks, pick[:near_windows], first, last))
    sizes = (len(far), z_parts, wins, chans, src_local)
    far_blocks = [v for g in far for v in g]
    return final_cross(sizes, far_blocks, parts, firsts, pick[near_windows:], rate)


def solution(mesh):
    return jax.shard_map(
        whole_step,
        mesh=mesh,
        in_specs=(P("tw", ("grp", "rx"), None), P("grp", None), P(None, "grp")),
        out_specs=P(("tw", "fq"), ("grp", "rx"), None),
        check_vma=False,
    )
```
